32 devices in a mesh: rep: 4 (over z), shard: 8 (over y, x, core).
Axes of the slice: x: 2, y: 2, z: 4, core: 2. Of those that a mesh axis runs over, the one named last changes fastest.
Arguments:
- stream_input: bfloat16 [64, 96, 1024], P(('rep', 'shard')), may hold values from -6 to 6
- output_cotangent: bfloat16 [64, 96, 1024], P(('rep', 'shard')), may hold values from -6 to 6
- image_mask: int32 [64], P(('rep', 'shard')), may hold values 0 or 1
- first_gain: bfloat16 [2, 1024], P(None, 'shard'), may hold values from 0.5 to 1.5
- first_shift: bfloat16 [2, 1024], P(None, 'shard'), may hold values from -0.59765625 to 0.59765625
- query_matrix: bfloat16 [2, 1024, 1024], P(None, 'shard'), may hold values from -0.25 to 0.25
- query_offset: bfloat16 [2, 1024], P(None, 'shard'), may hold values from -0.59765625 to 0.59765625
- key_matrix: bfloat16 [2, 1024, 1024], P(None, 'shard'), may hold values from -0.1875 to 0.1875
- value_matrix: bfloat16 [2, 1024, 1024], P(None, 'shard'), may hold values from -0.1875 to 0.1875
- value_offset: bfloat16 [2, 1024], P(None, 'shard'), may hold values from -0.59765625 to 0.59765625
- out_matrix: bfloat16 [2, 1024, 1024], P(None, 'shard'), may hold values from -0.75 to 0.75
- out_offset: bfloat16 [2, 1024], P(None, 'shard'), may hold values from -0.59765625 to 0.59765625
- second_gain: bfloat16 [2, 1024], P(None, 'shard'), may hold values from 0.5 to 1.5
- second_shift: bfloat16 [2, 1024], P(None, 'shard'), may hold values from -0.59765625 to 0.59765625
- expand_matrix: bfloat16 [2, 1024, 4096], P(None, 'shard'), may hold values from -0.1875 to 0.1875
- expand_offset: bfloat16 [2, 4096], P(None, 'shard'), may hold values from -0.59765625 to 0.59765625
- reduce_matrix: bfloat16 [2, 4096, 1024], P(None, 'shard'), may hold values from -0.125 to 0.125
- reduce_offset: bfloat16 [2, 1024], P(None, 'shard'), may hold values from -0.59765625 to 0.59765625
Outputs:
- stream_output: bfloat16 [64, 96, 1024], P(('rep', 'shard'))
- input_grad: float32 [64, 96, 1024], P(('rep', 'shard'))
- grad_first_gain: float32 [2, 1024], P(None, 'shard')
- grad_first_shift: float32 [2, 1024], P(None, 'shard')
- grad_query_matrix: float32 [2, 1024, 1024], P(None, 'shard')
- grad_query_offset: float32 [2, 1024], P(None, 'shard')
- grad_key_matrix: float32 [2, 1024, 1024], P(None, 'shard')
- grad_value_matrix: float32 [2, 1024, 1024], P(None, 'shard')
- grad_value_offset: float32 [2, 1024], P(None, 'shard')
- grad_out_matrix: float32 [2, 1024, 1024], P(None, 'shard')
- grad_out_offset: float32 [2, 1024], P(None, 'shard')
- grad_second_gain: float32 [2, 1024], P(None, 'shard')
- grad_second_shift: float32 [2, 1024], P(None, 'shard')
- grad_expand_matrix: float32 [2, 1024, 4096], P(None, 'shard')
- grad_expand_offset: float32 [2, 4096], P(None, 'shard')
- grad_reduce_matrix: float32 [2, 4096, 1024], P(None, 'shard')
- grad_reduce_offset: float32 [2, 1024], P(None, 'shard')
The draws below stay inside these ranges and needn't reach their ends.
Inputs may be any that keep to these rules, and one draw needn't show every extreme that they name: image_mask holds only 0 and 1.
All inputs are finite; a program needn't handle non-finite values. No bound on the sum of `image_mask` on one device may be relied on, other than what follows from the above.
Results may differ from the reference program's by a relative error of at most 0.025.
Values may be sent and summed in bfloat16 or wider, within the bound.
No kernel may reach another device: no remote copies, remote signals or barrier semaphores. Data moves between devices by JAX's collectives and lax.ppermute only.
A program may use at most 320 MiB of HBM per device.

```python
import math
import jax
import jax.numpy as jnp
from jax import lax

D = 1024
HEADS = 16
HEAD_DIM = 64
FF = 4096
LAYERS = 2
SEQ = 96
IMAGES = 64


def plant(entries, own_key, least, largest):
    spot = [jax.random.randint(jax.random.fold_in(own_key, axis), (), 0, length) for axis, length in enumerate(entries.shape)]
    widest = entries.shape.index(max(entries.shape))
    beside = spot[:widest] + [(spot[widest] + 1) % entries.shape[widest]] + spot[widest + 1:]
    return entries.at[tuple(spot)].set(least).at[tuple(beside)].set(largest)


def spiked(values, key, source, target, parts, factor):
    def block_of(dim):
        return (jnp.arange(values.shape[dim]) // (values.shape[dim] // parts)).reshape((-1,) + (1,) * (values.ndim - 1 - dim))

    first = jax.random.permutation(key, parts)[block_of(target)]
    second = (block_of(target) + parts // 2) % parts
    return jnp.where((block_of(source) == first) | (block_of(source) == second), factor * values, values)


def steps_of(rng, extent, pieces, smallest, high):
    def one(dim, shards_of):
        draws = jax.random.uniform(jax.random.fold_in(jax.random.fold_in(rng, 6), dim), (shards_of,), jnp.float32, smallest / len(pieces), high / len(pieces))
        return jnp.repeat(jnp.exp(draws), extent[dim] // shards_of).reshape((-1,) + (1,) * (len(extent) - dim - 1))

    loudness = one(*pieces[0])
    for cut in pieces[1:]:
        loudness = loudness * one(*cut)
    return loudness


def gaussian(rng, extent, deviation, bound, pieces=(), dtype=jnp.bfloat16):
    level = steps_of(rng, extent, pieces, -0.22, 0.18) if pieces else 1.0
    array = jax.random.normal(rng, extent, jnp.float32) * deviation * level
    return jnp.minimum(jnp.maximum(array, -bound), bound).astype(dtype)


def bell_draw_with(own_key, dims, deviation, most, split, heavy, kind=jnp.bfloat16):
    values = deviation * jax.random.normal(own_key, dims, jnp.float32)
    if split:
        values = values * steps_of(own_key, dims, split, -0.22, 0.18)
    return jnp.clip(spiked(values, jax.random.fold_in(own_key, 3), *heavy), -most, most).astype(kind)


def setup_inputs(seed: int = 0) -> dict:
    key_list = jax.random.split(jax.random.key(seed), 19)
    stream_input = gaussian(key_list[0], (IMAGES, SEQ, D), 1.0, 6.0, ((0, 32),))
    output_cotangent = bell_draw_with(key_list[1], (IMAGES, SEQ, D), 1.0, 6.0, ((0, 32),), (0, 2, 32, 2.75))
    image_mask = plant((jax.random.randint(key_list[2], (IMAGES,), 0, 8) < 7).astype(jnp.int32), jax.random.fold_in(key_list[2], 1), 0, 1)
    first_gain = jnp.clip(1.0 + 0.1 * jax.random.normal(key_list[3], (LAYERS, D), jnp.float32), 0.5, 1.5).astype(jnp.bfloat16)
    first_shift = gaussian(key_list[4], (LAYERS, D), 0.1, 0.59765625, ((1, 8),))
    query_matrix = gaussian(key_list[5], (LAYERS, D, D), (D // 2) ** -0.5, 0.25, ((1, 8),))
    query_offset = gaussian(key_list[6], (LAYERS, D), 0.1, 0.59765625, ((1, 8),))
    key_matrix = gaussian(key_list[7], (LAYERS, D, D), D ** -0.5, 0.1875, ((1, 8),))
    value_matrix = gaussian(key_list[8], (LAYERS, D, D), D ** -0.5, 0.1875, ((1, 8),))
    value_offset = gaussian(key_list[9], (LAYERS, D), 0.1, 0.59765625, ((1, 8),))
    out_matrix = gaussian(key_list[10], (LAYERS, D, D), (D // 16) ** -0.5, 0.75, ((1, 8),))
    out_offset = gaussian(key_list[11], (LAYERS, D), 0.1, 0.59765625, ((1, 8),))
    second_gain = jnp.clip(1.0 + 0.1 * jax.random.normal(key_list[12], (LAYERS, D), jnp.float32), 0.5, 1.5).astype(jnp.bfloat16)
    second_shift = gaussian(key_list[13], (LAYERS, D), 0.1, 0.59765625, ((1, 8),))
    expand_matrix = gaussian(key_list[14], (LAYERS, D, FF), D ** -0.5, 0.1875, ((1, 8),))
    expand_offset = gaussian(key_list[15], (LAYERS, FF), 0.1, 0.59765625, ((1, 8),))
    reduce_matrix = gaussian(key_list[16], (LAYERS, FF, D), (FF // 2) ** -0.5, 0.125, ((1, 8),))
    reduce_offset = gaussian(key_list[17], (LAYERS, D), 0.1, 0.59765625, ((1, 8),))
    return {"stream_input": stream_input, "output_cotangent": output_cotangent, "image_mask": image_mask, "first_gain": first_gain, "first_shift": first_shift, "query_matrix": query_matrix, "query_offset": query_offset, "key_matrix": key_matrix, "value_matrix": value_matrix, "value_offset": value_offset, "out_matrix": out_matrix, "out_offset": out_offset, "second_gain": second_gain, "second_shift": second_shift, "expand_matrix": expand_matrix, "expand_offset": expand_offset, "reduce_matrix": reduce_matrix, "reduce_offset": reduce_offset}


@jax.custom_vjp
def low(v):
    return lax.optimization_barrier(v.astype(jnp.bfloat16)).astype(jnp.float32)

@jax.custom_vjp
def low_back(v):
    return v

def low_keep(v):
    return (low(v), None)

def low_pass(kept, grad):
    return (grad,)

def back_keep(v):
    return (v, None)

def back_low(kept, grad):
    return (low(grad),)
low.defvjp(low_keep, low_pass)
low_back.defvjp(back_keep, back_low)
epsilon = 1e-05

def matmul(left, right):
    return jnp.dot(left, right, precision=lax.Precision.HIGHEST)

def normalize(values, gain, shift):
    center = values - lax.optimization_barrier(jnp.mean(values, axis=-1, keepdims=True))
    spread = lax.optimization_barrier(jnp.mean(center * center, axis=-1, keepdims=True))
    return center * lax.rsqrt(spread + epsilon) * gain + shift

def attend(queries, keys, values):
    length = queries.shape[0]
    heads_q = queries.reshape(length, HEADS, HEAD_DIM)
    heads_k = keys.reshape(length, HEADS, HEAD_DIM)
    heads_v = values.reshape(length, HEADS, HEAD_DIM)
    scores = jnp.einsum('qhd,khd->hqk', heads_q, heads_k, precision=lax.Precision.HIGHEST) * HEAD_DIM ** (-0.5)
    scores = low_back(scores)
    probs = low(jax.nn.softmax(scores, axis=-1))
    mixed = jnp.einsum('hqk,khd->qhd', probs, heads_v, precision=lax.Precision.HIGHEST)
    return mixed.reshape(length, HEADS * HEAD_DIM)

def layer(stream, weights):
    gain_one, shift_one, query_w, query_b, key_w, value_w, value_b, out_w, out_b, gain_two, shift_two, expand_w, expand_b, reduce_w, reduce_b = weights
    normed = low(normalize(stream, gain_one, shift_one))
    queries = low(low_back(matmul(normed, query_w) + query_b))
    keys = low(low_back(matmul(normed, key_w)))
    values = low(low_back(matmul(normed, value_w) + value_b))
    mixed = low(low_back(jax.vmap(attend)(queries, keys, values)))
    middle = stream + low_back(matmul(mixed, out_w) + out_b)
    normed_two = low(normalize(middle, gain_two, shift_two))
    hidden = low_back(matmul(normed_two, expand_w) + expand_b)
    active = low(hidden * jax.nn.sigmoid(1.702 * hidden))
    return middle + low_back(matmul(active, reduce_w) + reduce_b)

def forward(stream, params, maskf):
    for layer_index in range(LAYERS):
        stream = layer(stream, tuple((piece[layer_index] for piece in params)))
    return stream * maskf[:, None, None]

def reference(stream_input, output_cotangent, image_mask, first_gain, first_shift, query_matrix, query_offset, key_matrix, value_matrix, value_offset, out_matrix, out_offset, second_gain, second_shift, expand_matrix, expand_offset, reduce_matrix, reduce_offset):
    params = tuple((piece.astype(jnp.float32) for piece in (first_gain, first_shift, query_matrix, query_offset, key_matrix, value_matrix, value_offset, out_matrix, out_offset, second_gain, second_shift, expand_matrix, expand_offset, reduce_matrix, reduce_offset)))
    group = math.gcd(IMAGES, 2 ** int(math.log2(max(1, 4096 // SEQ))))
    count = IMAGES // group
    inputs = stream_input.astype(jnp.float32).reshape(count, group, SEQ, D)
    tangents = output_cotangent.astype(jnp.float32).reshape(count, group, SEQ, D)
    masks = image_mask.astype(jnp.float32).reshape(count, group)

    def step(total, item):
        block_in, block_tangent, block_mask = item
        result, pull = jax.vjp(lambda a, b: forward(a, b, block_mask), block_in, params)
        grad_in, grad_params = pull(block_tangent)
        total = jax.tree.map(jnp.add, total, grad_params)
        return (total, (result.astype(jnp.bfloat16), grad_in))
    zeros = tuple((jnp.zeros_like(piece) for piece in params))
    total, (results, grads_in) = lax.scan(step, zeros, (inputs, tangents, masks))
    return (results.reshape(IMAGES, SEQ, D), grads_in.reshape(IMAGES, SEQ, D), total[0], total[1], total[2], total[3], total[4], total[5], total[6], total[7], total[8], total[9], total[10], total[11], total[12], total[13], total[14])
```

```python
import functools

import jax
import jax.numpy as jnp
from jax import lax
from jax.experimental import pallas as pl
from jax.experimental.pallas import tpu as pltpu
from jax.sharding import PartitionSpec as P

HEADS = 16
HEAD_DIM = 64
LAYERS = 2
LANES = 128
EPSILON = 1e-05
FACTOR = HEAD_DIM ** (-0.5)
F32 = jnp.float32
BF16 = jnp.bfloat16


def dot(left, right):
    return lax.dot_general(left, right, (((1,), (0,)), ((), ())), preferred_element_type=F32)


def dot_left(left, right):
    return lax.dot_general(left, right, (((0,), (0,)), ((), ())), preferred_element_type=F32)


def dot_right(left, right):
    return lax.dot_general(left, right, (((1,), (1,)), ((), ())), preferred_element_type=F32)


LIMIT = 12


def call(name, body, outs, args, flops, limit=LIMIT, scratch=()):
    moved = sum(a.size * a.dtype.itemsize for a in args)
    moved += sum(o.size * o.dtype.itemsize for o in outs)
    spec = pl.BlockSpec(memory_space=pltpu.VMEM)
    return pl.pallas_call(
        body,
        out_shape=outs,
        in_specs=[spec] * len(args),
        out_specs=[spec] * len(outs),
        scratch_shapes=scratch,
        name=name,
        compiler_params=pltpu.CompilerParams(vmem_limit_bytes=limit << 20),
        cost_estimate=pl.CostEstimate(flops=int(flops), bytes_accessed=int(moved), transcendentals=0),
    )(*args)


def shape(rows, columns, kind):
    return jax.ShapeDtypeStruct((rows, columns), kind)


def head_masks(length):
    lane = lax.broadcasted_iota(jnp.int32, (length, LANES), 1)
    count = LANES // HEAD_DIM
    return [
        ((lane >= h * HEAD_DIM) & (lane < (h + 1) * HEAD_DIM)).astype(F32).astype(BF16)
        for h in range(count)
    ]


def softmax_of(queries, keys):
    scores = dot_right(queries, keys) * FACTOR
    raised = jnp.exp(scores - jnp.max(scores, axis=-1, keepdims=True))
    return raised / jnp.sum(raised, axis=-1, keepdims=True)


def attend(queries, keys, values, masks):
    mixed = None
    for mask in masks:
        probs = softmax_of(queries * mask, keys).astype(BF16)
        part = dot(probs, values * mask)
        mixed = part if mixed is None else mixed + part
    return mixed.astype(BF16)


def attend_back(queries, keys, values, upstream, masks):
    back_q = back_k = back_v = None
    for mask in masks:
        query_h = queries * mask
        upstream_h = upstream * mask
        probs = softmax_of(query_h, keys)
        back_probs = dot_right(upstream_h, values)
        delta = jnp.sum(probs * back_probs, axis=-1, keepdims=True)
        back_scores = (probs * (back_probs - delta)).astype(BF16)
        part_v = dot_left(probs.astype(BF16), upstream_h)
        part_q = dot(back_scores, keys * mask)
        part_k = dot_left(back_scores, query_h)
        back_q = part_q if back_q is None else back_q + part_q
        back_k = part_k if back_k is None else back_k + part_k
        back_v = part_v if back_v is None else back_v + part_v
    return (
        (back_q * FACTOR).astype(BF16),
        (back_k * FACTOR).astype(BF16),
        back_v.astype(BF16),
    )


GROUP = 4


def attention(qkv, length, width):
    rows = qkv.shape[0]
    steps = width // (LANES * GROUP)
    spec = lambda part: pl.BlockSpec((length, LANES * GROUP), lambda i, j: (i, part * steps + j))

    def body(q_ref, k_ref, v_ref, o_ref):
        masks = head_masks(length)
        for block in range(GROUP):
            here = slice(block * LANES, (block + 1) * LANES)
            o_ref[:, here] = attend(q_ref[:, here], k_ref[:, here], v_ref[:, here], masks)

    return pl.pallas_call(
        body,
        grid=(rows // length, steps),
        out_shape=shape(rows, width, BF16),
        in_specs=[spec(0), spec(1), spec(2)],
        out_specs=spec(0),
        name="attn_fwd",
        compiler_params=pltpu.CompilerParams(vmem_limit_bytes=LIMIT << 20),
        cost_estimate=pl.CostEstimate(
            flops=4 * rows * length * width, bytes_accessed=8 * rows * width, transcendentals=0
        ),
    )(qkv, qkv, qkv)


def attention_back(qkv, upstream, length, width):
    rows = qkv.shape[0]
    steps = width // (LANES * GROUP)
    spec = lambda part: pl.BlockSpec((length, LANES * GROUP), lambda i, j: (i, part * steps + j))

    def body(q_ref, k_ref, v_ref, u_ref, dq_ref, dk_ref, dv_ref):
        masks = head_masks(length)
        for block in range(GROUP):
            here = slice(block * LANES, (block + 1) * LANES)
            dq_ref[:, here], dk_ref[:, here], dv_ref[:, here] = attend_back(
                q_ref[:, here], k_ref[:, here], v_ref[:, here], u_ref[:, here], masks
            )

    return pl.pallas_call(
        body,
        grid=(rows // length, steps),
        out_shape=[shape(rows, width, BF16)] * 3,
        in_specs=[spec(0), spec(1), spec(2), spec(0)],
        out_specs=[spec(0)] * 3,
        name="attn_bwd",
        compiler_params=pltpu.CompilerParams(vmem_limit_bytes=LIMIT << 20),
        cost_estimate=pl.CostEstimate(
            flops=10 * rows * length * width, bytes_accessed=14 * rows * width, transcendentals=0
        ),
    )(qkv, qkv, qkv, upstream)


def heads_forward(pair, wqkv, bias, wo, length):
    rows, width = pair[0].shape
    wide = wqkv.shape[1]
    third = wide // 3

    def body(a_ref, b_ref, w_ref, bias_ref, wo_ref, pa_ref, pb_ref, qkv_ref, o_ref):
        masks = head_masks(length)
        for at, (h_ref, p_ref) in enumerate(((a_ref, pa_ref), (b_ref, pb_ref))):
            base = at * rows
            qkv_ref[base : base + rows, :] = (dot(h_ref[...], w_ref[...]) + bias_ref[...]).astype(
                BF16
            )
            for image in range(rows // length):
                here = slice(base + image * length, base + (image + 1) * length)
                o_ref[here, :] = attend(
                    qkv_ref[here, 0:third],
                    qkv_ref[here, third : 2 * third],
                    qkv_ref[here, 2 * third :],
                    masks,
                )
            p_ref[...] = dot(o_ref[base : base + rows, :], wo_ref[...]).astype(BF16)

    return call(
        "heads_fwd",
        body,
        [
            shape(rows, width, BF16),
            shape(rows, width, BF16),
            shape(2 * rows, wide, BF16),
            shape(2 * rows, third, BF16),
        ],
        [pair[0], pair[1], wqkv, bias, wo],
        4 * rows * width * (wide + third),
    )


def heads_backward(pair, qkv, wqkv, wo, length):
    rows, width = pair[0].shape
    wide = wqkv.shape[1]
    third = wide // 3

    def body(a_ref, b_ref, qkv_ref, w_ref, wo_ref, pa_ref, pb_ref, d_ref):
        masks = head_masks(length)
        for at, (h_ref, p_ref) in enumerate(((a_ref, pa_ref), (b_ref, pb_ref))):
            base = at * rows
            back = dot_right(h_ref[...], wo_ref[...]).astype(BF16)
            for image in range(rows // length):
                here = slice(base + image * length, base + (image + 1) * length)
                dq, dk, dv = attend_back(
                    qkv_ref[here, 0:third],
                    qkv_ref[here, third : 2 * third],
                    qkv_ref[here, 2 * third :],
                    back[image * length : (image + 1) * length, :],
                    masks,
                )
                d_ref[here, 0:third] = dq
                d_ref[here, third : 2 * third] = dk
                d_ref[here, 2 * third :] = dv
            p_ref[...] = dot_right(d_ref[base : base + rows, :], w_ref[...]).astype(BF16)

    return call(
        "heads_bwd",
        body,
        [shape(rows, width, BF16), shape(rows, width, BF16), shape(2 * rows, wide, BF16)],
        [pair[0], pair[1], qkv, wqkv, wo],
        4 * rows * width * (wide + third),
    )


def feed_forward(pair, we, bias, wr):
    rows, width = pair[0].shape
    units = we.shape[1]

    def body(a_ref, b_ref, we_ref, bias_ref, wr_ref, pa_ref, pb_ref, u_ref, g_ref):
        for at, (h_ref, p_ref) in enumerate(((a_ref, pa_ref), (b_ref, pb_ref))):
            base = at * rows
            hidden = dot(h_ref[...], we_ref[...]) + bias_ref[...]
            u_ref[base : base + rows, :] = hidden
            active = (hidden * jax.nn.sigmoid(1.702 * hidden)).astype(BF16)
            g_ref[base : base + rows, :] = active
            p_ref[...] = dot(active, wr_ref[...]).astype(BF16)

    return call(
        "feed_fwd",
        body,
        [
            shape(rows, width, BF16),
            shape(rows, width, BF16),
            shape(2 * rows, units, F32),
            shape(2 * rows, units, BF16),
        ],
        [pair[0], pair[1], we, bias, wr],
        8 * rows * width * units,
    )


def feed_backward(pair, hidden, we, wr):
    rows, width = pair[0].shape
    units = we.shape[1]

    def body(a_ref, b_ref, u_ref, we_ref, wr_ref, pa_ref, pb_ref, d_ref):
        for at, (h_ref, p_ref) in enumerate(((a_ref, pa_ref), (b_ref, pb_ref))):
            base = at * rows
            back = dot_right(h_ref[...], wr_ref[...])
            u = u_ref[base : base + rows, :]
            sigma = jax.nn.sigmoid(1.702 * u)
            low = (back * (sigma + 1.702 * u * sigma * (1.0 - sigma))).astype(BF16)
            d_ref[base : base + rows, :] = low
            p_ref[...] = dot_right(low, we_ref[...]).astype(BF16)

    return call(
        "feed_bwd",
        body,
        [shape(rows, width, BF16), shape(rows, width, BF16), shape(2 * rows, units, BF16)],
        [pair[0], pair[1], hidden, we, wr],
        8 * rows * width * units,
    )


def joined_product(lefts, rights):
    depth = sum(left.shape[0] for left in lefts)
    high, wide = lefts[0].shape[1], rights[0].shape[1]
    step = min(high, 128)

    def body(*refs):
        left_refs, right_refs = refs[: len(lefts)], refs[len(lefts) : len(lefts) + len(rights)]
        out_ref, left_all, right_all = refs[len(lefts) + len(rights) :]
        for pieces, whole in ((left_refs, left_all), (right_refs, right_all)):
            at = 0
            for piece in pieces:
                whole[at : at + piece.shape[0], :] = piece[...]
                at += piece.shape[0]

        for first in range(0, high, step):
            here = slice(first, first + step)
            out_ref[here, :] = dot_left(left_all[:, here], right_all[...]).astype(BF16)

    return call(
        "wgrad",
        body,
        [shape(high, wide, BF16)],
        [*lefts, *rights],
        2 * depth * high * wide,
        scratch=[pltpu.VMEM((depth, high), BF16), pltpu.VMEM((depth, wide), BF16)],
    )[0]


def token_product(first, first_right, second, second_right, columns):
    rows, width = first.shape
    one, two, three = first_right.shape[1], second_right.shape[1], columns.shape[1]
    step = 128

    def body(a_ref, ar_ref, b_ref, br_ref, c_ref, out_ref):
        out_ref[:, 0:one] = dot_left(a_ref[...], ar_ref[...]).astype(BF16)
        out_ref[:, one : one + two] = dot_left(b_ref[...], br_ref[...]).astype(BF16)
        out_ref[:, one + two :] = c_ref[...].astype(BF16)

    tall = pl.BlockSpec((rows, step), lambda i: (0, i))
    fixed = lambda wide: pl.BlockSpec((rows, wide), lambda i: (0, 0))
    return pl.pallas_call(
        body,
        grid=(width // step,),
        out_shape=shape(width, one + two + three, BF16),
        in_specs=[tall, fixed(one), tall, fixed(two), pl.BlockSpec((step, three), lambda i: (i, 0))],
        out_specs=pl.BlockSpec((step, one + two + three), lambda i: (i, 0)),
        name="token_grad",
        compiler_params=pltpu.CompilerParams(vmem_limit_bytes=LIMIT << 20),
        cost_estimate=pl.CostEstimate(
            flops=2 * rows * width * (one + two),
            bytes_accessed=2 * width * (one + two + three),
            transcendentals=0,
        ),
    )(first, first_right, second, second_right, columns)


CHUNK = 32


def normal(values):
    center = values - jnp.mean(values, axis=-1, keepdims=True)
    inverse = lax.rsqrt(jnp.mean(center * center, axis=-1, keepdims=True) + EPSILON)
    return center * inverse, inverse


def norm_forward(stream, parts, vecs, offset, gain, shift):
    rows, width = stream.shape
    count = len(parts)

    def body(*refs):
        x_ref, part_refs, vec_ref = refs[0], refs[1 : 1 + count], refs[1 + count]
        out_refs = refs[2 + count :]

        @pl.loop(0, rows // CHUNK)
        def _(step):
            here = pl.ds(pl.multiple_of(step * CHUNK, CHUNK), CHUNK)
            total = x_ref[here, :].astype(F32)
            if count:
                added = part_refs[0][here, :].astype(F32)
                for ref in part_refs[1:]:
                    added = added + ref[here, :].astype(F32)
                total = total + (added + vec_ref[offset : offset + 1, :])
                out_refs[0][here, :] = total
            scaled, _ = normal(total)
            out_refs[-1][here, :] = (
                scaled * vec_ref[gain : gain + 1, :] + vec_ref[shift : shift + 1, :]
            ).astype(BF16)

    outs = [shape(rows, width, BF16)]
    if count:
        outs = [shape(rows, width, F32)] + outs
    return call("norm_fwd", body, outs, [stream, *parts, vecs], 10 * rows * width)


def norm_backward(parts, through, stream, vecs, gain, low):
    rows, width = stream.shape
    count = len(parts)

    def body(*refs):
        part_refs, c_ref, x_ref, vec_ref = refs[:count], refs[count], refs[count + 1], refs[count + 2]
        d_ref, sum_ref = refs[count + 3], refs[count + 4]
        sum_ref[...] = jnp.zeros_like(sum_ref)

        @pl.loop(0, rows // CHUNK)
        def _(step):
            here = pl.ds(pl.multiple_of(step * CHUNK, CHUNK), CHUNK)
            upstream = part_refs[0][here, :].astype(F32)
            for ref in part_refs[1:]:
                upstream = upstream + ref[here, :].astype(F32)
            scaled, inverse = normal(x_ref[here, :].astype(F32))
            slope = upstream * vec_ref[gain : gain + 1, :]
            inner = (
                slope
                - jnp.mean(slope, axis=-1, keepdims=True)
                - scaled * jnp.mean(slope * scaled, axis=-1, keepdims=True)
            )
            result = c_ref[here, :].astype(F32) + inner * inverse
            d_ref[here, :] = result
            sum_ref[0:1, :] += jnp.sum(upstream * scaled, axis=0, keepdims=True)
            sum_ref[1:2, :] += jnp.sum(upstream, axis=0, keepdims=True)
            if low:
                rounded = result.astype(BF16)
                refs[count + 5][here, :] = rounded
                sum_ref[2:3, :] += jnp.sum(rounded.astype(F32), axis=0, keepdims=True)

    outs = [shape(rows, width, F32), shape(8, width, F32)]
    if low:
        outs = outs + [shape(rows, width, BF16)]
    return call("norm_bwd", body, outs, [*parts, through, stream, vecs], 20 * rows * width)


def shards(
    size,
    stream_input,
    output_cotangent,
    image_mask,
    first_gain,
    first_shift,
    query_matrix,
    query_offset,
    key_matrix,
    value_matrix,
    value_offset,
    out_matrix,
    out_offset,
    second_gain,
    second_shift,
    expand_matrix,
    expand_offset,
    reduce_matrix,
    reduce_offset,
):
    images, length, width = stream_input.shape
    rows = images * length
    wide = width // LANES
    inner = size // wide
    outer_groups = [[t * inner + r for t in range(wide)] for r in range(inner)]
    inner_groups = [[t * inner + r for r in range(inner)] for t in range(wide)]
    me = lax.axis_index("shard")

    def swap(value, distance):
        return lax.ppermute(value, "shard", [(i, i ^ (distance * inner)) for i in range(size)])

    def share(value):
        if inner == 1:
            return value
        return lax.all_gather(value, "shard", axis=0, tiled=True, axis_index_groups=inner_groups)

    def unshare(value):
        if inner == 1:
            return value
        return lax.psum_scatter(
            value, "shard", scatter_dimension=0, tiled=True, axis_index_groups=inner_groups
        )

    def rows_to_columns(value):
        return lax.all_to_all(
            value, "shard", split_axis=1, concat_axis=0, tiled=True, axis_index_groups=outer_groups
        )

    def columns_to_rows(value):
        return lax.all_to_all(
            value, "shard", split_axis=0, concat_axis=1, tiled=True, axis_index_groups=outer_groups
        )

    def gather(block):
        even = [block] + [swap(block, k) for k in range(2, wide, 2)]
        blocks = []
        for one in even:
            blocks += [one, swap(one, 1)]
        return blocks

    def scatter(parts):
        even = []
        for k in range(0, wide, 2):
            total = parts[k].astype(F32) + swap(parts[k + 1], 1).astype(F32)
            even.append(total.astype(BF16))
        return [even[0]] + [swap(even[k // 2], k) for k in range(2, wide, 2)]

    def together(*values):
        return lax.optimization_barrier(values)

    replicas = lax.axis_size("rep")
    middle = (lax.axis_index("rep") == 1) | (lax.axis_index("rep") == 2)

    def add(one, other):
        return (one.astype(F32) + other.astype(F32)).astype(one.dtype)

    def inward(value):
        if replicas != 4:
            return lax.psum(value, "rep")
        return add(value, lax.ppermute(value, "rep", [(0, 1), (3, 2)]))

    def across(value):
        if replicas != 4:
            return value
        return add(value, lax.ppermute(value, "rep", [(1, 2), (2, 1)]))

    def outward(value):
        if replicas != 4:
            return value
        return jnp.where(middle, value, lax.ppermute(value, "rep", [(1, 0), (2, 3)]))

    def pairs(blocks):
        return [(blocks[k], blocks[k + 1]) for k in range(0, wide, 2)]

    def staged(stage, blocks, *rest):
        done = [stage(pair, *(r[i] if isinstance(r, list) else r for r in rest)) for i, pair in enumerate(pairs(blocks))]
        parts = [part for result in done for part in result[:2]]
        others = [list(kind) for kind in zip(*(result[2:] for result in done))]
        return parts, *others

    join = lambda pieces: jnp.concatenate(pieces, axis=0)

    names = (first_gain, first_shift, out_offset, second_gain, second_shift, reduce_offset)
    pieces = [vector[layer] for layer in range(LAYERS) for vector in names]
    pieces += [query_offset[1], value_offset[1]]
    count = len(pieces)
    vecs = lax.all_gather(jnp.concatenate(pieces), "shard", axis=0, tiled=False)
    vecs = vecs.reshape(size, count, -1).transpose(1, 0, 2).reshape(count, width).astype(F32)
    at = lambda layer, which: layer * len(names) + which

    heads = [share(m[0]).reshape(-1, wide, LANES) for m in (query_matrix, key_matrix, value_matrix)]
    wqkv = rows_to_columns(jnp.stack(heads, axis=2).reshape(-1, 3 * width))
    wo = share(out_matrix[0])
    zero = jnp.zeros((LANES,), BF16)
    bias_qkv = jnp.concatenate([share(query_offset[0]), zero, share(value_offset[0])])
    bias_qkv = bias_qkv.astype(F32)[None, :]
    we = [rows_to_columns(share(expand_matrix[layer])) for layer in range(LAYERS)]
    wr = [share(reduce_matrix[layer]) for layer in range(LAYERS)]
    bias_u = [share(expand_offset[layer]).astype(F32)[None, :] for layer in range(LAYERS)]
    whole = jnp.concatenate([query_matrix[1], key_matrix[1], value_matrix[1], out_matrix[1]], axis=1)
    whole = lax.all_gather(whole, "shard", axis=0, tiled=True)
    whole_qkv, whole_out = whole[:, : 3 * width], whole[:, 3 * width :]
    bias_whole = jnp.concatenate([vecs[count - 2], jnp.zeros((width,), F32), vecs[count - 1]])

    maskf = jnp.broadcast_to(image_mask.astype(F32)[:, None], (images, length)).reshape(rows, 1)
    x0 = stream_input.reshape(rows, width)
    top = output_cotangent.astype(F32).reshape(rows, width) * maskf
    dm1 = top.astype(BF16)

    (h1,) = norm_forward(x0, [], vecs, None, at(0, 0), at(0, 1))
    h1s = gather(h1)
    parts, qkv0, o0 = staged(lambda pair: heads_forward(pair, wqkv, bias_qkv, wo, length), h1s)
    x1, h2 = norm_forward(x0, scatter(parts), vecs, at(0, 2), at(0, 3), at(0, 4))
    x1, h2, we[0] = together(x1, h2, we[0])
    h2s = gather(h2)
    parts, u0, g0 = staged(lambda pair: feed_forward(pair, we[0], bias_u[0], wr[0]), h2s)
    x2, h3 = norm_forward(x1, scatter(parts), vecs, at(0, 5), at(1, 0), at(1, 1))
    x2, h3, we[1] = together(x2, h3, we[1])

    qkv1 = (dot(h3, whole_qkv) + bias_whole).astype(BF16)
    o1 = attention(qkv1, length, width)
    x3, h4 = norm_forward(x2, [dot(o1, whole_out)], vecs, at(1, 2), at(1, 3), at(1, 4))
    x3, h4, *dms = together(x3, h4, *gather(dm1))
    h4s = gather(h4)
    parts, u1, g1 = staged(lambda pair: feed_forward(pair, we[1], bias_u[1], wr[1]), h4s)

    backs, du1 = staged(lambda pair, u: feed_backward(pair, u, we[1], wr[1]), dms, u1)
    grad_reduce1 = joined_product(g1, dms)
    grad_expand1 = joined_product(h4s, du1)
    d3, sums_d3, da1 = norm_backward(scatter(backs), top, x3, vecs, at(1, 3), True)
    d3, sums_d3, da1, grad_reduce1, grad_expand1 = together(
        d3, sums_d3, da1, grad_reduce1, grad_expand1
    )
    grad_reduce1 = unshare(grad_reduce1)
    grad_expand1 = unshare(columns_to_rows(grad_expand1))
    back_o = dot_right(da1, whole_out).astype(BF16)
    dqkv1 = jnp.concatenate(attention_back(qkv1, back_o, length, width), axis=1)
    d2, sums_d2, dm0 = norm_backward([dot_right(dqkv1, whole_qkv)], d3, x2, vecs, at(1, 0), True)
    grad_reduce1 = lax.psum(grad_reduce1, "rep")
    d2, sums_d2, dm0, grad_reduce1, grad_expand1 = together(
        d2, sums_d2, dm0, grad_reduce1, grad_expand1
    )
    grad_expand1 = lax.psum(grad_expand1, "rep")

    last = scatter(parts)
    total = last[0].astype(F32)
    for piece in last[1:]:
        total = total + piece.astype(F32)
    output = ((x3 + (total + vecs[at(1, 5)])) * maskf).astype(BF16).reshape(images, length, width)

    column_sum = lambda value: jnp.sum(value.astype(F32), axis=0)[None, :]
    sums_qkv1 = column_sum(dqkv1).reshape(3, width)
    early = jnp.concatenate(
        [sums_d2[0:2], sums_qkv1, sums_d3[2:3], sums_d3[0:2], column_sum(dm1)], axis=0
    )
    early = jnp.pad(early, ((0, LANES - early.shape[0]), (0, 0))).T
    grad_whole1 = token_product(h3, dqkv1, o1, da1, early)

    *dms0, grad_whole1 = together(*gather(dm0), grad_whole1)
    grad_whole1 = lax.psum_scatter(grad_whole1, "shard", scatter_dimension=0, tiled=True)
    backs, du0 = staged(lambda pair, u: feed_backward(pair, u, we[0], wr[0]), dms0, u0)
    grad_reduce0 = joined_product(g0, dms0)
    grad_expand0 = joined_product(h2s, du0)
    d1, sums_d1, da0 = norm_backward(scatter(backs), d2, x1, vecs, at(0, 3), True)
    d1, sums_d1, da0, grad_reduce0, grad_expand0 = together(
        d1, sums_d1, da0, grad_reduce0, grad_expand0
    )
    grad_reduce0 = inward(unshare(grad_reduce0))
    grad_expand0 = unshare(columns_to_rows(grad_expand0))
    *das, grad_expand1, grad_reduce0 = together(*gather(da0), grad_expand1, grad_reduce0)
    grad_expand0 = inward(grad_expand0)
    grad_reduce0 = across(grad_reduce0)
    backs, dqkv0 = staged(lambda pair, qkv: heads_backward(pair, qkv, wqkv, wo, length), das, qkv0)
    *dqkv0, grad_expand1, grad_whole1 = together(*dqkv0, grad_expand1, grad_whole1)
    grad_whole1 = lax.psum(grad_whole1, "rep")
    *dqkv0, grad_expand0, grad_reduce0 = together(*dqkv0, grad_expand0, grad_reduce0)
    grad_qkv0 = unshare(columns_to_rows(joined_product(h1s, dqkv0))).reshape(-1, wide, 3, LANES)
    grad_out0 = inward(unshare(joined_product(o0, das)))
    grad_reduce0 = outward(grad_reduce0)
    grad_expand0 = across(grad_expand0)
    grad_qkv0, grad_expand0, grad_reduce0, grad_out0 = together(
        grad_qkv0, grad_expand0, grad_reduce0, grad_out0
    )
    third = lambda which: outward(across(inward(grad_qkv0[:, :, which, :].reshape(-1, width))))
    grad_query0, grad_key0, grad_value0 = third(0), third(1), third(2)
    grad_expand0 = outward(grad_expand0)
    grad_out0 = outward(across(grad_out0))
    d0, sums_d0 = norm_backward(scatter(backs), d1, x0, vecs, at(0, 0), False)

    lines = jnp.concatenate([sums_d0[0:2], sums_d1[2:3], sums_d1[0:2], sums_d2[2:3]])
    if inner == 1:
        lines = lines.reshape(-1, wide, LANES).transpose(1, 0, 2)
        lines = jnp.sum(lax.all_to_all(lines, "shard", split_axis=0, concat_axis=0), axis=0)
    else:
        lines = lax.psum_scatter(lines, "shard", scatter_dimension=1, tiled=True)
    own = [*column_sum(join(dqkv0)).reshape(3, LANES), column_sum(join(du0))[0], column_sum(join(du1))[0]]
    own = jnp.concatenate([unshare(value) for value in own]).reshape(-1, width // size)
    late = lax.psum(jnp.concatenate([lines, own]), "rep")

    early_part = grad_whole1[:, 4 * width :].astype(F32).T
    stack = lambda low, high: jnp.stack([low.astype(F32), high.astype(F32)])
    vector = lambda low, high: jnp.stack([late[low], early_part[high]])
    block = lambda which: grad_whole1[:, which * width : (which + 1) * width]
    return (
        output,
        d0.reshape(images, length, width),
        vector(0, 0),
        vector(1, 1),
        stack(grad_query0, block(0)),
        vector(6, 2),
        stack(grad_key0, block(1)),
        stack(grad_value0, block(2)),
        vector(8, 4),
        stack(grad_out0, block(3)),
        vector(2, 5),
        vector(3, 6),
        vector(4, 7),
        stack(grad_expand0, grad_expand1),
        jnp.stack([late[9:13].reshape(-1), late[13:17].reshape(-1)]),
        stack(grad_reduce0, grad_reduce1),
        vector(5, 8),
    )


def solution(mesh):
    tokens = P(("rep", "shard"), None, None)
    vector = P(None, "shard")
    matrix = P(None, "shard", None)
    params = (
        vector, vector, matrix, vector, matrix, matrix, vector, matrix,
        vector, vector, vector, matrix, vector, matrix, vector,
    )
    return jax.shard_map(
        functools.partial(shards, mesh.shape["shard"]),
        mesh=mesh,
        in_specs=(tokens, tokens, P(("rep", "shard"))) + params,
        out_specs=(tokens, tokens) + params,
        check_vma=False,
    )
```
